32 devices in a mesh: band: 8 (over z, core), row: 4 (over y, x).
Axes of the slice: x: 2, y: 2, z: 4, core: 2. Of those that a mesh axis runs over, the one named last changes fastest.
Arguments:
- valence_store: bfloat16 [64, 16384], P('band', 'row'), may hold values from -6 to 6
- valence_energy: float32 [12], replicated, may hold values from -10 to -0.01
- owners: int32 [3], replicated, may hold values from 0 to 7
- occupancy: int32 [12], replicated, may hold values from 1 to 2
- conduction: bfloat16 [384, 16384], P('band'), may hold values from -6 to 6
- cond_energy: float32 [384], replicated, may hold values from 0.01 to 10
Outputs:
- chi: float32 [1024, 16384], P('band', 'row')
The draws below stay inside these ranges and needn't reach their ends.
Inputs may be any that keep to these rules, and one draw needn't show every extreme that they name: owners[g] is the index of band whose stored rows hold valence group g, in slot g mod 2.
All inputs are finite; a program needn't handle non-finite values.
Results may differ from the reference program's by a relative error of at most 0.0003.
Values may be sent and summed in bfloat16 or wider, within the bound.
No kernel may reach another device: no remote copies, remote signals or barrier semaphores. Data moves between devices by JAX's collectives and lax.ppermute only.
A program may use at most 64 MiB of HBM per device.

```python
import math
import jax
import jax.numpy as jnp
from jax import lax

NMU = 16384
VG = 4
NGROUP = 3
SLOTS = 2
NV = 12
NC = 384
QWIN = 1024
NSTORE = 64
N_BAND = 8


def draw_valence_energy(key, part):
    level = jax.random.uniform(key, (NV,), jnp.float32, math.log(0.01), math.log(10.0))
    return (-jnp.exp(level)).astype(jnp.float32)


def touch_ends(values, own_key, least, top_value):
    index_at = [jax.random.randint(jax.random.fold_in(own_key, axis), (), 0, length) for axis, length in enumerate(values.shape)]
    main_axis = values.shape.index(max(values.shape))
    beside = index_at[:main_axis] + [(index_at[main_axis] + 1) % values.shape[main_axis]] + index_at[main_axis + 1:]
    return values.at[tuple(index_at)].set(least).at[tuple(beside)].set(top_value)


def block_scale(key, shape, cuts, least, high):
    def one(position, blocks):
        heights = jax.random.uniform(jax.random.fold_in(jax.random.fold_in(key, 6), position), (blocks,), jnp.float32, least / len(cuts), high / len(cuts))
        return jnp.repeat(jnp.exp(heights), shape[position] // blocks).reshape((-1,) + (1,) * (len(shape) - position - 1))

    factor_of = one(*cuts[0])
    for cut in cuts[1:]:
        factor_of = factor_of * one(*cut)
    return factor_of


def centred(rng, dims, spread, bound, cuts=(), kind=jnp.bfloat16):
    gain = block_scale(rng, dims, cuts, -0.22, 0.18) if cuts else 1.0
    drawn = jax.random.normal(rng, dims, jnp.float32) * spread * gain
    return jnp.minimum(jnp.maximum(drawn, -bound), bound).astype(kind)


def setup_inputs(seed: int = 0) -> dict:
    key_of = jax.random.split(jax.random.key(seed), 7)
    valence_store = centred(key_of[0], (NSTORE, NMU), 1.0, 6.0, ((0, 8), (1, 4)))
    valence_energy = draw_valence_energy(jax.random.fold_in(key_of[6], 71), 0)
    owners = jax.random.randint(key_of[2], (NGROUP,), 0, N_BAND).astype(jnp.int32)
    occupancy = touch_ends(jax.random.randint(key_of[3], (NV,), 1, 3), jax.random.fold_in(key_of[3], 1), 1, 2).astype(jnp.int32)
    conduction = centred(key_of[4], (NC, NMU), 1.0, 6.0, ((0, 8),))
    cond_energy = jnp.clip(jnp.exp(jax.random.uniform(key_of[5], (NC,), jnp.float32, math.log(0.01), math.log(10.0))), 0.01, 10.0)
    return {"valence_store": valence_store, "valence_energy": valence_energy, "owners": owners, "occupancy": occupancy, "conduction": conduction, "cond_energy": cond_energy}


def reference(valence_store, valence_energy, owners, occupancy, conduction, cond_energy):
    group_slot = (jnp.arange(NGROUP, dtype=jnp.int32) % SLOTS).astype(jnp.int32)
    starts = ((owners * SLOTS + group_slot) * VG).astype(jnp.int32)
    index = (starts[:, None] + jnp.arange(VG, dtype=jnp.int32)[None, :]).reshape(-1)
    chosen = jnp.take(valence_store, index, axis=0).astype(jnp.float32)
    weight = occupancy.astype(jnp.float32)[:, None] / (valence_energy[:, None] - cond_energy[None, :])
    cond_full = conduction.astype(jnp.float32)
    cond_window = cond_full[:, :QWIN]

    def step(total, items):
        val_row, weight_row = items
        left = (val_row[None, :QWIN] * cond_window) * weight_row[:, None]
        right = val_row[None, :] * cond_full
        product = jnp.dot(left.T, right, precision=lax.Precision.HIGHEST)
        return total + product, None

    total, _ = lax.scan(step, jnp.zeros((QWIN, NMU), jnp.float32), (chosen, weight))
    return total * (4.0 / (NC * NV) ** 0.5)
```

```python
import math

import jax
import jax.numpy as jnp
from jax import lax
from jax.experimental import pallas as pl
from jax.experimental.pallas import tpu as pltpu
from jax.sharding import PartitionSpec as P

QDEV = 128
VG = 4
NGROUP = 3
SLOTS = 2
NV = 12
HALVES = 2
KCHIP = 256
TILE = 512


def ring_order(chips):
    order = [0] + list(range(1, chips, 2)) + list(range(chips - 2, 0, -2))
    return order


def prep_kernel(me_ref, window_ref, val_ref, weight_ref, left_ref, cols_ref):
    cores = window_ref.shape[0]
    cond_local = window_ref.shape[1]
    chips = cores // 2
    half = KCHIP // 2
    cols_ref[...] = jnp.zeros_like(cols_ref)
    for block in range(cores):
        band = me_ref[0] ^ block
        start = (band // 2) * half + (band % 2) * cond_local
        cols_ref[pl.ds(pl.multiple_of(start, 16), cond_local), :] = window_ref[block].astype(jnp.float32)
    val = val_ref[...].astype(jnp.float32).T
    for chip in range(chips):
        cond = cols_ref[chip * half : (chip + 1) * half, :].T
        for band in range(NV):
            weight = weight_ref[band : band + 1, chip * half : (chip + 1) * half]
            left = (val[:, band : band + 1] * cond) * weight
            high = left.astype(jnp.bfloat16)
            low = (left - high.astype(jnp.float32)).astype(jnp.bfloat16)
            rows = slice(band * QDEV, (band + 1) * QDEV)
            left_ref[chip, rows, :half] = high
            left_ref[chip, rows, half:] = low


def prepare(me, window, val, weight):
    cores, cond_local, _ = window.shape
    chips = cores // 2
    return pl.pallas_call(
        prep_kernel,
        out_shape=jax.ShapeDtypeStruct((chips, NV * QDEV, KCHIP), jnp.bfloat16),
        in_specs=[pl.BlockSpec(memory_space=pltpu.SMEM)] + [pl.BlockSpec(memory_space=pltpu.VMEM)] * 3,
        out_specs=pl.BlockSpec(memory_space=pltpu.VMEM),
        scratch_shapes=[pltpu.VMEM((chips * KCHIP // 2, QDEV), jnp.float32)],
        compiler_params=pltpu.CompilerParams(vmem_limit_bytes=40 * 2**20),
        name="prep",
    )(me, window, val, weight)


def product(steps, info, left, streams, values, acc, offset):
    count = len(steps)
    cond_local = streams[0][0].shape[0]
    width = streams[0][0].shape[1]
    half = KCHIP // 2
    first = acc is None

    def kernel(info_ref, *refs):
        left_refs = refs[:count]
        stream_refs = refs[count : 3 * count]
        rest = refs[3 * count :]
        value_ref = rest[0]
        right_ref = rest[-1]
        out_ref = rest[-2]

        @pl.when(pl.program_id(0) == 0)
        def _():
            right_ref[...] = jnp.zeros_like(right_ref)

        core = info_ref[0]
        for step in range(count):
            for part in range(2):
                for lane in range(2):
                    where = jnp.where(core == lane, 0, cond_local)
                    start = step * KCHIP + part * half + where
                    right_ref[pl.ds(pl.multiple_of(start, 16), cond_local), :] = stream_refs[2 * step + lane][...]
        total = None
        for band in range(0, NV, VG):
            m = None
            for step in range(count):
                piece = jnp.dot(
                    left_refs[step][0, band * QDEV : (band + VG) * QDEV, :],
                    right_ref[step * KCHIP : (step + 1) * KCHIP, :],
                    preferred_element_type=jnp.float32,
                )
                m = piece if m is None else m + piece
            for j in range(VG):
                value = value_ref[band + j : band + j + 1, :].astype(jnp.float32)
                term = m[j * QDEV : (j + 1) * QDEV] * value
                total = term if total is None else total + term
        if first:
            out_ref[...] = total
        else:
            out_ref[...] = rest[1][...] + total

    def left_spec(step):
        return pl.BlockSpec((1, NV * QDEV, KCHIP), lambda i, info: (info[1 + step], 0, 0))

    tile = pl.BlockSpec((cond_local, TILE), lambda i, info: (0, i))
    in_specs = [left_spec(step) for step in steps] + [tile] * (2 * count)
    first_tile = offset // TILE
    in_specs.append(pl.BlockSpec((NV, TILE), lambda i, info: (0, first_tile + i)))
    operands = [left] * count + [x for pair in streams for x in pair] + [values]
    if not first:
        in_specs.append(pl.BlockSpec((QDEV, TILE), lambda i, info: (0, i)))
        operands.append(acc)
    return pl.pallas_call(
        kernel,
        out_shape=jax.ShapeDtypeStruct((QDEV, width), jnp.float32),
        grid_spec=pltpu.PrefetchScalarGridSpec(
            num_scalar_prefetch=1,
            grid=(width // TILE,),
            in_specs=in_specs,
            out_specs=pl.BlockSpec((QDEV, TILE), lambda i, info: (0, i)),
            scratch_shapes=[pltpu.VMEM((count * KCHIP, TILE), jnp.bfloat16)],
        ),
        compiler_params=pltpu.CompilerParams(vmem_limit_bytes=40 * 2**20),
        name="product",
    )(info, *operands)


def body(valence_store, valence_energy, owners, occupancy, conduction, cond_energy):
    band_count = lax.axis_size("band")
    row_count = lax.axis_size("row")
    band_index = lax.axis_index("band")
    row_index = lax.axis_index("row")
    chips = band_count // 2
    chip = band_index // 2
    core = band_index % 2
    point_rows = valence_store.shape[1]
    cond_local = conduction.shape[0]
    window = QDEV * band_count
    width = point_rows // HALVES

    order = ring_order(chips)
    follow = {order[i]: order[(i + 1) % chips] for i in range(chips)}
    before = [0] * chips
    for source, target in follow.items():
        before[target] = source
    ring = [(c * 2 + k, follow[c] * 2 + k) for c in range(chips) for k in range(2)]
    sibling = [(i, i ^ 1) for i in range(band_count)]

    before = jnp.array(before, jnp.int32)
    sources = [chip]
    for _ in range(chips - 1):
        sources.append(before[sources[-1]])
    info = jnp.stack([core] + sources).astype(jnp.int32)

    own = []
    for h in range(HALVES):
        own.append(
            lax.dynamic_slice_in_dim(conduction, row_index * point_rows + h * width, width, 1)
        )
    stream = [own]
    for _ in range(chips - 1):
        stream.append([lax.ppermute(x, "band", ring) for x in stream[-1]])
    other = [[lax.ppermute(x, "band", sibling) for x in xs] for xs in stream]

    near = jnp.where(row_index == 0, valence_store[:, :window], jnp.zeros((), valence_store.dtype))
    bit = 1
    while bit < row_count:
        near = near + lax.ppermute(near, "row", [(i, i + bit) for i in range(bit)])
        bit *= 2

    def selected(store):
        groups = []
        for group in range(NGROUP):
            first = group % SLOTS * VG
            piece = store[first : first + VG]
            groups.append(jnp.where(band_index == owners[group], piece, jnp.zeros_like(piece)))
        return jnp.concatenate(groups, axis=0)

    values = selected(valence_store)
    split = point_rows // 2
    keep = lax.dynamic_slice_in_dim(values, core * split, split, 1)
    send = lax.dynamic_slice_in_dim(values, (1 - core) * split, split, 1)
    keep = keep + lax.ppermute(send, "band", sibling)

    cols = conduction[:, :window]
    vals = selected(near)
    bit = band_count // 2
    while bit >= 1:
        size = cols.shape[1] // 2
        mine = (band_index // bit) % 2
        perm = [(i, i ^ bit) for i in range(band_count)]
        both = jnp.concatenate([cols, vals], axis=0)
        part = lax.dynamic_slice_in_dim(both, mine * size, size, 1)
        away = lax.dynamic_slice_in_dim(both, (1 - mine) * size, size, 1)
        got = lax.ppermute(away, "band", perm)
        rows = cols.shape[0]
        cols = jnp.concatenate([part[:rows], got[:rows]], axis=0)
        vals = part[rows:] + got[rows:]
        if bit >= 2:
            keep = keep + lax.ppermute(keep, "band", perm)
        bit //= 2
    away = lax.ppermute(keep, "band", sibling)
    values = jnp.where(
        core == 0, jnp.concatenate([keep, away], axis=1), jnp.concatenate([away, keep], axis=1)
    )

    bits = int(math.log2(band_count))
    cols = cols.reshape((2,) * bits + (cond_local, QDEV))
    cols = cols.reshape(band_count, cond_local, QDEV)
    place = [0] * band_count
    for block in range(band_count):
        mask = 0
        for j in range(bits):
            if (block >> (bits - 1 - j)) & 1:
                mask |= 1 << j
        place[mask] = block
    cols = jnp.stack([cols[place[mask]] for mask in range(band_count)])

    scale = 4.0 / math.sqrt(cond_local * band_count * NV)
    occupied = occupancy.astype(jnp.float32)
    weight = occupied[:, None] / (valence_energy[:, None] - cond_energy[None, :])
    weight = weight.reshape(NV, chips, 2 * cond_local)
    weight = jnp.pad(weight, ((0, 0), (0, 0), (0, KCHIP // 2 - 2 * cond_local)))
    weight = weight.reshape(NV, chips * KCHIP // 2)
    left = prepare(band_index.astype(jnp.int32)[None], cols, vals, weight * scale)

    outs = []
    for h in range(HALVES):
        pairs = [(stream[s][h], other[s][h]) for s in range(chips)]
        acc = product(list(range(chips - 1)), info, left, pairs[:-1], values, None, h * width)
        acc = product([chips - 1], info, left, pairs[-1:], values, acc, h * width)
        outs.append(acc)
    return jnp.concatenate(outs, axis=1)


def solution(mesh):
    in_specs = (P("band", "row"), P(), P(), P(), P("band", None), P())
    out_specs = P("band", "row")
    return jax.shard_map(body, mesh=mesh, in_specs=in_specs, out_specs=out_specs, check_vma=False)
```

```python
import math

import jax
import jax.numpy as jnp
from jax import lax
from jax.experimental import pallas as pl
from jax.experimental.pallas import tpu as pltpu
from jax.sharding import PartitionSpec as P

QDEV = 128
VG = 4
NGROUP = 3
SLOTS = 2
NV = 12
NVPAD = 16
KCHIP = 256
LAST = 2
TILE = 512
VMEM_LIMIT = 40 * 2**20
BF16 = jnp.bfloat16
F32 = jnp.float32

HBM = pl.BlockSpec(memory_space=pltpu.HBM)
VMEM = pl.BlockSpec(memory_space=pltpu.VMEM)


def ring_order(chips):
    return [0] + list(range(1, chips, 2)) + list(range(chips - 2, 0, -2))


def previous(chips):
    order = ring_order(chips)
    return [order[order.index(c) - 1] for c in range(chips)]


def lookup(table, index):
    value = jnp.int32(table[0])
    for i in range(1, len(table)):
        value = jnp.where(index == i, jnp.int32(table[i]), value)
    return value


def call(kernel, name, operands, in_specs, out_shape, out_specs, scratch=(), aliases=None, carry=()):
    ins, outs, carried = len(operands), len(out_shape), len(carry)

    def body(*refs):
        rest = refs[ins + carried :]
        kernel(*refs[:ins], *rest[:outs], *rest[outs + carried :])

    aliases = dict(aliases or {})
    for i in range(carried):
        aliases[ins + i] = outs + i
    results = pl.pallas_call(
        body,
        out_shape=list(out_shape) + [jax.ShapeDtypeStruct(x.shape, x.dtype) for x in carry],
        in_specs=list(in_specs) + [VMEM] * carried,
        out_specs=list(out_specs) + [VMEM] * carried,
        scratch_shapes=list(scratch),
        input_output_aliases=aliases,
        compiler_params=pltpu.CompilerParams(vmem_limit_bytes=VMEM_LIMIT),
        name=name,
    )(*operands, *carry)
    return list(results[:outs]), list(results[outs:])


def pinned(x):
    return pltpu.with_memory_space_constraint(x, pltpu.HBM)


def nearby(store, window, lead):
    def kernel(store_ref, lead_ref, out_ref, sem):
        copy = pltpu.make_async_copy(store_ref.at[:, :window], out_ref, sem)
        copy.start()
        copy.wait()

        @pl.when(lax.axis_index("row") != 0)
        def _():
            out_ref[...] = jnp.zeros_like(out_ref)

    shape = jax.ShapeDtypeStruct((store.shape[0], window), BF16)
    outs, _ = call(
        kernel,
        "nearby",
        [pinned(store), lead],
        [HBM, VMEM],
        [shape],
        [VMEM],
        [pltpu.SemaphoreType.DMA],
    )
    return outs[0]


def cut(owners, store, conduction, nears, chips, carry):
    points = store.shape[1]
    cond_local = conduction.shape[0]
    blocks = points // 256

    def kernel(owners_ref, store_ref, cond_ref, *refs):
        near_refs = refs[: len(nears)]
        refs = refs[len(nears) :]
        pieces = refs[:chips]
        keep_ref, send_ref, rows_ref, group_ref, sems = refs[chips:]
        band = lax.axis_index("band")
        chip = band // 2
        core = band % 2
        copies = [
            pltpu.make_async_copy(store_ref, rows_ref, sems.at[0]),
            pltpu.make_async_copy(owners_ref, group_ref, sems.at[1]),
        ]
        for m in range(chips):
            for k in range(2):
                start = ((chip ^ m) * 2 + k) * QDEV
                copies.append(
                    pltpu.make_async_copy(
                        cond_ref.at[:, pl.ds(pl.multiple_of(start, QDEV), QDEV)],
                        pieces[m].at[k * cond_local : (k + 1) * cond_local],
                        sems.at[2 + 2 * m + k],
                    )
                )
        for copy in copies:
            copy.start()
        copies[0].wait()
        copies[1].wait()

        def chosen(rows):
            parts = []
            for group in range(NGROUP):
                first = group % SLOTS * VG
                part = rows[first : first + VG]
                parts.append(jnp.where(band == group_ref[group], part, 0.0))
            return jnp.concatenate(parts, axis=0).astype(BF16)

        for k, ref in ((core, keep_ref), (1 - core, send_ref)):
            for block in range(blocks):
                lanes = pl.ds(pl.multiple_of(block * 256 + k * QDEV, QDEV), QDEV)
                rows = rows_ref[:, lanes].astype(F32)
                ref[block * NV : (block + 1) * NV, :] = chosen(rows)
            for c in range(chips):
                lanes = pl.ds(pl.multiple_of(c * 256 + k * QDEV, QDEV), QDEV)
                rows = near_refs[0][:, lanes].astype(F32)
                for near_ref in near_refs[1:]:
                    rows = rows + near_ref[:, lanes].astype(F32)
                ref[(blocks + c) * NV : (blocks + c + 1) * NV, :] = chosen(rows)
        for copy in copies[2:]:
            copy.wait()

    piece = jax.ShapeDtypeStruct((2 * cond_local, QDEV), BF16)
    share = jax.ShapeDtypeStruct(((blocks + chips) * NV, QDEV), BF16)
    outs, carried = call(
        kernel,
        "cut",
        [pinned(x) for x in (owners, store, conduction)] + nears,
        [HBM] * 3 + [VMEM] * len(nears),
        [piece] * chips + [share] * 2,
        [VMEM] * (chips + 2),
        [
            pltpu.VMEM(store.shape, BF16),
            pltpu.SMEM(owners.shape, jnp.int32),
            pltpu.SemaphoreType.DMA((2 + 2 * chips,)),
        ],
        carry=carry,
    )
    return outs[:chips], outs[chips], outs[chips + 1], carried


def spread(keep, got, pieces, share, carry):
    chips = len(pieces)
    first = pieces[0].shape[0]

    def kernel(keep_ref, got_ref, *refs):
        chip = lax.axis_index("band") // 2
        total = keep_ref[...].astype(F32) + got_ref[...].astype(F32)
        for m in range(chips):
            out_ref = refs[chips + m]
            near = jnp.zeros((NV, QDEV), F32)
            for c in range(chips):
                block = total[share + c * NV : share + (c + 1) * NV]
                near = jnp.where(c == (chip ^ m), block, near)
            out_ref[:first] = refs[m][...]
            out_ref[first : first + share] = total[:share].astype(BF16)
            near = jnp.concatenate([near, jnp.zeros((NVPAD - NV, QDEV), F32)], axis=0)
            out_ref[first + share :] = near.astype(BF16)

    shape = jax.ShapeDtypeStruct((first + share + NVPAD, QDEV), BF16)
    return call(
        kernel,
        "spread",
        [keep, got, *pieces],
        [VMEM] * (2 + chips),
        [shape] * chips,
        [VMEM] * chips,
        carry=carry,
    )


def pack(windows, share, first, carry):
    chips = len(windows)
    cond_local = first // 2

    def kernel(*refs):
        window_refs = refs[:chips]
        out_ref, near_ref = refs[chips:]
        core = lax.axis_index("band") % 2
        total = window_refs[0][first:].astype(F32)
        for ref in window_refs[1:]:
            total = total + ref[first:].astype(F32)
        out_ref[:share] = total[:share].astype(BF16)
        near_ref[...] = total[share:].astype(BF16)
        for m in range(chips):
            start = pl.multiple_of((1 - core) * cond_local, 16)
            out_ref[share + m * cond_local : share + (m + 1) * cond_local] = window_refs[m][
                pl.ds(start, cond_local)
            ]

    return call(
        kernel,
        "pack",
        windows,
        [VMEM] * chips,
        [
            jax.ShapeDtypeStruct((share + chips * cond_local, QDEV), BF16),
            jax.ShapeDtypeStruct((NVPAD, QDEV), BF16),
        ],
        [VMEM] * 2,
        carry=carry,
    )


def gate(token, carry):
    def kernel(token_ref):
        pass

    return call(kernel, "gate", [token], [VMEM], [], [], carry=carry)[1]


def prepare(weight, packed, got, windows, near, share, first, carry):
    chips = len(windows)
    cond_local = first // 2
    half = KCHIP // 2
    blocks = share // NV

    def kernel(weight_ref, packed_ref, got_ref, near_ref, *refs):
        window_refs = refs[:chips]
        left_ref, values_ref, token_ref, cols_ref = refs[chips:]
        token_ref[...] = jnp.zeros_like(token_ref)
        band = lax.axis_index("band")
        chip = band // 2
        core = band % 2
        for block in range(blocks):
            rows = slice(block * NV, (block + 1) * NV)
            for k, ref in ((core, packed_ref), (1 - core, got_ref)):
                lanes = pl.ds(pl.multiple_of(block * 256 + k * QDEV, QDEV), QDEV)
                values_ref[:NV, lanes] = ref[rows].astype(F32)
        cols_ref[...] = jnp.zeros_like(cols_ref)
        for m in range(chips):
            base = (chip ^ m) * half
            mine = core * cond_local
            cols_ref[pl.ds(pl.multiple_of(base + core * cond_local, 16), cond_local)] = window_refs[m][
                pl.ds(pl.multiple_of(mine, 16), cond_local)
            ].astype(F32)
            theirs = slice(share + m * cond_local, share + (m + 1) * cond_local)
            cols_ref[pl.ds(pl.multiple_of(base + (1 - core) * cond_local, 16), cond_local)] = got_ref[
                theirs
            ].astype(F32)
        near = near_ref[...].astype(F32).T
        for c in range(chips):
            cond = cols_ref[c * half : (c + 1) * half, :].T
            for v in range(NV):
                left = (near[:, v : v + 1] * cond) * weight_ref[v : v + 1, c * half : (c + 1) * half]
                high = left.astype(BF16)
                low = (left - high.astype(F32)).astype(BF16)
                rows = slice(v * QDEV, (v + 1) * QDEV)
                left_ref[c, rows, :half] = high
                left_ref[c, rows, half:] = low

    return call(
        kernel,
        "prep",
        [weight, packed, got, near] + windows,
        [VMEM] * (4 + chips),
        [
            jax.ShapeDtypeStruct((chips, NV * QDEV, KCHIP), BF16),
            jax.ShapeDtypeStruct((NVPAD, blocks * 256), F32),
            jax.ShapeDtypeStruct((8, 128), F32),
        ],
        [VMEM] * 3,
        [pltpu.VMEM((chips * half, QDEV), F32)],
        carry=carry,
    )


def product(steps, chips, left, streams, values, acc, offset, width, out, points, carry):
    count = len(steps)
    cond_local = streams[0][0].shape[0]
    half = KCHIP // 2
    before = previous(chips)
    tiles = width // TILE
    final = out is not False
    first = acc is None

    def kernel(left_ref, values_ref, *refs):
        stream_refs = refs[: 2 * count]
        rest = list(refs[2 * count :])
        acc_ref = None if first else rest.pop(0)
        if final and out is not None:
            rest.pop(0)
        out_ref, token_ref = rest[:2]
        token_ref[...] = jnp.zeros_like(token_ref)
        band = lax.axis_index("band")
        core = band % 2
        source = band // 2
        sources = [source]
        for _ in range(max(steps)):
            source = lookup(before, source)
            sources.append(source)

        copies = []
        for tile in range(tiles):
            lanes = slice(tile * TILE, (tile + 1) * TILE)

            def load(index, k):
                return stream_refs[2 * index + k][:, lanes]

            parts = []
            gap = jnp.zeros((half - 2 * cond_local, TILE), BF16)
            for index in range(count):
                mine = load(index, 0)
                theirs = load(index, 1)
                pair = [jnp.where(core == 0, mine, theirs), jnp.where(core == 0, theirs, mine), gap]
                parts += pair + pair
            right = jnp.concatenate(parts, axis=0)
            total = None if first else acc_ref[:, lanes]
            for v in range(0, NV, VG):
                rows = slice(v * QDEV, (v + VG) * QDEV)
                parts = [left_ref[sources[step], rows, :] for step in steps]
                lhs = parts[0] if count == 1 else jnp.concatenate(parts, axis=1)
                m = jnp.dot(lhs, right, preferred_element_type=F32)
                for j in range(VG):
                    value = values_ref[v + j : v + j + 1, offset + tile * TILE : offset + (tile + 1) * TILE]
                    term = m[j * QDEV : (j + 1) * QDEV] * value
                    total = term if total is None else total + term
            if final:
                stage_ref, sems = rest[2:]
                stage_ref[tile] = total
                copy = pltpu.make_async_copy(
                    stage_ref.at[tile],
                    out_ref.at[:, offset + tile * TILE : offset + (tile + 1) * TILE],
                    sems.at[tile],
                )
                copy.start()
                copies.append(copy)
            else:
                out_ref[:, lanes] = total
        for copy in copies:
            copy.wait()

    operands = [left, values] + [x for pair in streams for x in pair]
    in_specs = [VMEM] * len(operands)
    aliases = {}
    if not first:
        operands.append(acc)
        in_specs.append(VMEM)
        if not final:
            aliases = {len(operands) - 1: 0}
    scratch = []
    if final:
        if out is not None:
            operands.append(out)
            in_specs.append(HBM)
            aliases = {len(operands) - 1: 0}
        scratch = [pltpu.VMEM((tiles, QDEV, TILE), F32), pltpu.SemaphoreType.DMA((tiles,))]
        out_shape = jax.ShapeDtypeStruct((QDEV, points), F32)
        out_spec = HBM
    else:
        out_shape = jax.ShapeDtypeStruct((QDEV, width), F32)
        out_spec = VMEM
    return call(
        kernel,
        "product",
        operands,
        in_specs,
        [out_shape, jax.ShapeDtypeStruct((8, 128), F32)],
        [out_spec, VMEM],
        scratch,
        aliases,
        carry,
    )


def body(valence_store, valence_energy, owners, occupancy, conduction, cond_energy):
    band_count = lax.axis_size("band")
    row_count = lax.axis_size("row")
    window = QDEV * band_count
    row_index = lax.axis_index("row")
    chips = band_count // 2
    points = valence_store.shape[1]
    cond_local = conduction.shape[0]
    share = points // 256 * NV

    units = points // TILE
    widths = [TILE * (units - units // LAST)]
    widths.append(points - sum(widths))
    offsets = [0, widths[0]]
    chunks = range(len(widths))

    order = ring_order(chips)
    follow = {order[i]: order[(i + 1) % chips] for i in range(chips)}
    ring = [(c * 2 + k, follow[c] * 2 + k) for c in range(chips) for k in range(2)]
    sibling = [(i, i ^ 1) for i in range(band_count)]

    def swap(m):
        return [(i, i ^ (2 * m)) for i in range(band_count)]

    def forward(x):
        return lax.ppermute(x, "band", ring)

    def exchange(x):
        return lax.ppermute(x, "band", sibling)

    own = [
        lax.dynamic_slice_in_dim(conduction, row_index * points + offsets[h], widths[h], 1)
        for h in chunks
    ]
    arrived = [[None] * len(widths) for _ in range(chips)]
    stream = [[None] * len(widths) for _ in range(chips)]
    other = [[None] * len(widths) for _ in range(chips)]
    arrived[1] = [forward(x) for x in own]
    near = nearby(valence_store, window, own[0])
    nears = [near] + [lax.ppermute(near, "row", [(0, r)]) for r in range(1, row_count)]
    pieces, keep, send, (lead, *stream[0]) = cut(
        owners, valence_store, conduction, nears, chips, [arrived[1][0]] + own
    )
    got = exchange(send)
    beside = [exchange(x) for x in stream[0]]
    first = 2 * cond_local
    windows, (lead, last, *other[0]) = spread(
        keep, got, pieces, share, [lead, arrived[1][1]] + beside
    )
    for m in range(1, chips):
        windows[m] = lax.ppermute(windows[m], "band", swap(m))

    def send_on(s, h, carried):
        stream[s][h] = carried
        if s + 1 < chips:
            arrived[s + 1][h] = forward(carried)
        other[s][h] = exchange(carried)

    scale = 4.0 / math.sqrt(cond_local * band_count * NV)
    occupied = occupancy.astype(F32)
    weight = occupied[:, None] / (valence_energy[:, None] - cond_energy[None, :])
    weight = weight.reshape(NV, chips, 2 * cond_local) * scale
    weight = jnp.pad(weight, ((0, 0), (0, 0), (0, KCHIP // 2 - 2 * cond_local)))
    weight = weight.reshape(NV, chips * KCHIP // 2)

    send_on(1, 0, lead)
    send_on(1, 1, last)
    (packed, near), _ = pack(windows, share, first, ())
    theirs = exchange(packed)
    (left, values, token), _ = prepare(weight, packed, theirs, windows, near, share, first, ())

    out = None
    accs = [None] * len(widths)
    groups = [[0, 1]] + [[s] for s in range(2, chips)]
    waiting = [(s, h) for s in range(2, chips) for h in chunks]
    for group in groups:
        final = group[-1] == chips - 1
        for h in chunks:
            carry = []
            if waiting and (group[-1] < chips - 2 or h == 0):
                carry = [waiting.pop(0)]
            (result, _), carried = product(
                group,
                chips,
                left,
                [(stream[s][h], other[s][h]) for s in group],
                values,
                accs[h],
                offsets[h],
                widths[h],
                out if final else False,
                points,
                [arrived[s][n] for s, n in carry] + (accs[1:] if final and h == 0 else []),
            )
            if final and h == 0:
                accs[1:] = carried[len(carry) :]
            for (s, n), x in zip(carry, carried):
                send_on(s, n, x)
            if final:
                out = result
            else:
                accs[h] = result
    return out


def solution(mesh):
    in_specs = (P("band", "row"), P(), P(), P(), P("band", None), P())
    out_specs = P("band", "row")
    return jax.shard_map(body, mesh=mesh, in_specs=in_specs, out_specs=out_specs, check_vma=False)
```

```python
import math

import jax
import jax.numpy as jnp
from jax import lax
from jax.experimental import pallas as pl
from jax.experimental.pallas import tpu as pltpu
from jax.sharding import PartitionSpec as P

QDEV = 128
VG = 4
NGROUP = 3
SLOTS = 2
NV = 12
NVPAD = 16
KCHIP = 256
LAST = 2
TILE = 512
VMEM_LIMIT = 40 * 2**20
BF16 = jnp.bfloat16
F32 = jnp.float32

HBM = pl.BlockSpec(memory_space=pltpu.HBM)
VMEM = pl.BlockSpec(memory_space=pltpu.VMEM)


def ring_order(chips):
    return [0] + list(range(1, chips, 2)) + list(range(chips - 2, 0, -2))


def previous(chips):
    order = ring_order(chips)
    return [order[order.index(c) - 1] for c in range(chips)]


def lookup(table, index):
    value = jnp.int32(table[0])
    for i in range(1, len(table)):
        value = jnp.where(index == i, jnp.int32(table[i]), value)
    return value


def call(kernel, name, operands, in_specs, out_shape, out_specs, scratch=(), aliases=None, carry=()):
    ins, outs, carried = len(operands), len(out_shape), len(carry)

    def body(*refs):
        rest = refs[ins + carried :]
        kernel(*refs[:ins], *rest[:outs], *rest[outs + carried :])

    aliases = dict(aliases or {})
    for i in range(carried):
        aliases[ins + i] = outs + i
    results = pl.pallas_call(
        body,
        out_shape=list(out_shape) + [jax.ShapeDtypeStruct(x.shape, x.dtype) for x in carry],
        in_specs=list(in_specs) + [VMEM] * carried,
        out_specs=list(out_specs) + [VMEM] * carried,
        scratch_shapes=list(scratch),
        input_output_aliases=aliases,
        compiler_params=pltpu.CompilerParams(vmem_limit_bytes=VMEM_LIMIT),
        name=name,
    )(*operands, *carry)
    return list(results[:outs]), list(results[outs:])


def pinned(x):
    return pltpu.with_memory_space_constraint(x, pltpu.HBM)


def cut(store, conduction, nears, chips, carry):
    slots, points = store.shape
    cond_local = conduction.shape[0]
    first = 2 * cond_local
    blocks = points // QDEV

    def kernel(store_ref, cond_ref, *refs):
        near_refs = refs[: len(nears)]
        refs = refs[len(nears) :]
        outs = refs[:chips]
        rows_ref, sems = refs[chips:]
        chip = lax.axis_index("band") // 2
        copies = [pltpu.make_async_copy(store_ref, rows_ref, sems.at[0])]
        for m in range(chips):
            for k in range(2):
                start = ((chip ^ m) * 2 + k) * QDEV
                copies.append(
                    pltpu.make_async_copy(
                        cond_ref.at[:, pl.ds(pl.multiple_of(start, QDEV), QDEV)],
                        outs[m].at[k * cond_local : (k + 1) * cond_local],
                        sems.at[1 + 2 * m + k],
                    )
                )
        for copy in copies:
            copy.start()
        copies[0].wait()
        for block in range(blocks):
            rows = rows_ref[:, block * QDEV : (block + 1) * QDEV]
            for out_ref in outs:
                out_ref[first + block * slots : first + (block + 1) * slots, :] = rows
        for m in range(chips):
            for k in range(2):
                lanes = pl.ds(pl.multiple_of(((chip ^ m) * 2 + k) * QDEV, QDEV), QDEV)
                rows = near_refs[0][:, lanes].astype(F32)
                for ref in near_refs[1:]:
                    rows = rows + ref[:, lanes].astype(F32)
                start = first + (blocks + k) * slots
                outs[m][start : start + slots, :] = rows.astype(BF16)
        for copy in copies[1:]:
            copy.wait()

    shape = jax.ShapeDtypeStruct((first + (blocks + 2) * slots, QDEV), BF16)
    return call(
        kernel,
        "cut",
        [pinned(store), pinned(conduction)] + nears,
        [HBM] * 2 + [VMEM] * len(nears),
        [shape] * chips,
        [VMEM] * chips,
        [pltpu.VMEM(store.shape, BF16), pltpu.SemaphoreType.DMA((1 + 2 * chips,))],
        carry=carry,
    )


def pack(owners, windows, first, slots, carry):
    chips = len(windows)
    cond_local = first // 2
    blocks = (windows[0].shape[0] - first) // slots - 2
    share = blocks * NV

    def kernel(owners_ref, *refs):
        window_refs = refs[:chips]
        out_ref, near_ref, group_ref, sem = refs[chips:]
        copy = pltpu.make_async_copy(owners_ref, group_ref, sem)
        copy.start()
        band = lax.axis_index("band")
        core = band % 2
        for m in range(chips):
            start = pl.multiple_of((1 - core) * cond_local, 16)
            out_ref[share + m * cond_local : share + (m + 1) * cond_local] = window_refs[m][
                pl.ds(start, cond_local)
            ]
        copy.wait()
        def chosen(start):
            rows = [ref[pl.ds(start, slots), :].astype(F32) for ref in window_refs]
            parts = []
            for group in range(NGROUP):
                at = group % SLOTS * VG
                part = jnp.zeros((VG, QDEV), F32)
                for m in range(chips):
                    source = band ^ (2 * m)
                    part = jnp.where(source == group_ref[group], rows[m][at : at + VG], part)
                parts.append(part)
            return parts

        for block in range(blocks):
            rows = jnp.concatenate(chosen(first + block * slots), axis=0)
            out_ref[block * NV : (block + 1) * NV] = rows.astype(BF16)
        rest = [jnp.zeros((NVPAD - NV, QDEV), F32)]
        near = first + blocks * slots
        mine = jnp.concatenate(chosen(pl.multiple_of(near + core * slots, 8)) + rest, axis=0)
        near_ref[...] = mine.astype(BF16)
        theirs = jnp.concatenate(chosen(pl.multiple_of(near + (1 - core) * slots, 8)) + rest, axis=0)
        out_ref[share + chips * cond_local :] = theirs.astype(BF16)

    (packed, near), carried = call(
        kernel,
        "pack",
        [pinned(owners)] + windows,
        [HBM] + [VMEM] * chips,
        [
            jax.ShapeDtypeStruct((share + chips * cond_local + NVPAD, QDEV), BF16),
            jax.ShapeDtypeStruct((NVPAD, QDEV), BF16),
        ],
        [VMEM] * 2,
        [pltpu.SMEM(owners.shape, jnp.int32), pltpu.SemaphoreType.DMA],
        carry=carry,
    )
    return packed, near, carried


def nearby(store, window, lead):
    def kernel(store_ref, lead_ref, out_ref, sem):
        copy = pltpu.make_async_copy(store_ref.at[:, :window], out_ref, sem)
        copy.start()
        copy.wait()

        @pl.when(lax.axis_index("row") != 0)
        def _():
            out_ref[...] = jnp.zeros_like(out_ref)

    shape = jax.ShapeDtypeStruct((store.shape[0], window), BF16)
    outs, _ = call(
        kernel,
        "nearby",
        [pinned(store), lead],
        [HBM, VMEM],
        [shape],
        [VMEM],
        [pltpu.SemaphoreType.DMA],
    )
    return outs[0]


def gate(token, carry):
    def kernel(token_ref):
        pass

    return call(kernel, "gate", [token], [VMEM], [], [], carry=carry)[1]


def sources(chip, chips):
    before = previous(chips)
    found = [chip]
    for _ in range(chips - 1):
        found.append(lookup(before, found[-1]))
    return found


def prepare(weight, packed, got, windows, near, share, first, carry):
    chips = len(windows)
    cond_local = first // 2
    blocks = share // NV
    depth = chips * first

    def kernel(weight_ref, packed_ref, got_ref, near_ref, *refs):
        window_refs = refs[:chips]
        left_ref, values_ref, token_ref, cols_ref = refs[chips:]
        token_ref[...] = jnp.zeros_like(token_ref)
        band = lax.axis_index("band")
        chip = band // 2
        core = band % 2
        for block in range(blocks):
            rows = slice(block * NV, (block + 1) * NV)
            values = packed_ref[rows].astype(F32) + got_ref[rows].astype(F32)
            values_ref[:NV, block * QDEV : (block + 1) * QDEV] = values
        steps = sources(chip, chips)
        parts = []
        for source in steps:
            for k in (core, 1 - core):
                start = source * first + k * cond_local
                parts.append(weight_ref[pl.ds(pl.multiple_of(start, 8), cond_local), :])
        weights = jnp.concatenate(parts, axis=0).T
        for m in range(chips):
            step = jnp.int32(0)
            for s in range(1, chips):
                step = jnp.where(steps[s] == (chip ^ m), jnp.int32(s), step)
            base = step * first
            mine = core * cond_local
            cols_ref[pl.ds(pl.multiple_of(base, 16), cond_local)] = window_refs[m][
                pl.ds(pl.multiple_of(mine, 16), cond_local)
            ].astype(F32)
            theirs = slice(share + m * cond_local, share + (m + 1) * cond_local)
            cols_ref[pl.ds(pl.multiple_of(base + cond_local, 16), cond_local)] = got_ref[
                theirs
            ].astype(F32)
        near = near_ref[...].astype(F32) + got_ref[share + chips * cond_local :].astype(F32)
        near = near.T
        cond = cols_ref[...].T
        for v in range(NV):
            left = (near[:, v : v + 1] * cond) * weights[v : v + 1, :]
            high = left.astype(BF16)
            low = (left - high.astype(F32)).astype(BF16)
            rows = slice(v * QDEV, (v + 1) * QDEV)
            left_ref[rows, :depth] = high
            left_ref[rows, depth:] = low

    return call(
        kernel,
        "prep",
        [weight, packed, got, near] + windows,
        [VMEM] * (4 + chips),
        [
            jax.ShapeDtypeStruct((NV * QDEV, 2 * depth), BF16),
            jax.ShapeDtypeStruct((NVPAD, blocks * QDEV), F32),
            jax.ShapeDtypeStruct((8, 128), F32),
        ],
        [VMEM] * 3,
        [pltpu.VMEM((depth, QDEV), F32)],
        carry=carry,
    )


def product(begin, end, left, streams, values, acc, offset, out, points):
    count = len(streams)
    cond_local, width = streams[0].shape
    tiles = width // TILE
    half = left.shape[1] // 2
    start = 2 * begin * cond_local // QDEV * QDEV
    stop = -(-2 * end * cond_local // QDEV) * QDEV
    head = 2 * begin * cond_local - start
    tail = stop - 2 * end * cond_local
    final = out is not False

    def kernel(left_ref, values_ref, *refs):
        stream_refs = refs[:count]
        rest = list(refs[count:])
        acc_ref = None if acc is None else rest.pop(0)
        if final and out is not None:
            rest.pop(0)
        out_ref, token_ref = rest[:2]
        token_ref[...] = jnp.zeros_like(token_ref)
        copies = []
        for tile in range(tiles):
            lanes = slice(tile * TILE, (tile + 1) * TILE)
            at = slice(offset + tile * TILE, offset + (tile + 1) * TILE)
            parts = [ref[:, lanes] for ref in stream_refs]
            if head:
                parts = [jnp.zeros((head, TILE), BF16)] + parts
            if tail:
                parts = parts + [jnp.zeros((tail, TILE), BF16)]
            right = jnp.concatenate(parts + parts, axis=0)
            total = None if acc is None else acc_ref[:, lanes]
            for v in range(0, NV, VG):
                rows = slice(v * QDEV, (v + VG) * QDEV)
                lhs = jnp.concatenate(
                    [left_ref[rows, start:stop], left_ref[rows, half + start : half + stop]], axis=1
                )
                m = jnp.dot(lhs, right, preferred_element_type=F32)
                for j in range(VG):
                    term = m[j * QDEV : (j + 1) * QDEV] * values_ref[v + j : v + j + 1, at]
                    total = term if total is None else total + term
            if final:
                stage_ref, sems = rest[2:]
                stage_ref[tile] = total
                copy = pltpu.make_async_copy(stage_ref.at[tile], out_ref.at[:, at], sems.at[tile])
                copy.start()
                copies.append(copy)
            else:
                out_ref[:, lanes] = total
        for copy in copies:
            copy.wait()

    operands = [left, values] + streams
    in_specs = [VMEM] * len(operands)
    aliases = {}
    scratch = []
    if acc is not None:
        operands.append(acc)
        in_specs.append(VMEM)
    if final:
        if out is not None:
            operands.append(out)
            in_specs.append(HBM)
            aliases = {len(operands) - 1: 0}
        scratch = [pltpu.VMEM((tiles, QDEV, TILE), F32), pltpu.SemaphoreType.DMA((tiles,))]
    shape = (QDEV, points if final else width)
    outs, _ = call(
        kernel,
        "product",
        operands,
        in_specs,
        [jax.ShapeDtypeStruct(shape, F32), jax.ShapeDtypeStruct((8, 128), F32)],
        [HBM if final else VMEM, VMEM],
        scratch,
        aliases,
    )
    return outs


def body(valence_store, valence_energy, owners, occupancy, conduction, cond_energy):
    band_count = lax.axis_size("band")
    row_count = lax.axis_size("row")
    row_index = lax.axis_index("row")
    chips = band_count // 2
    points = valence_store.shape[1]
    cond_local = conduction.shape[0]
    share = points // QDEV * NV

    units = points // TILE
    widths = [TILE * (units - units // LAST)]
    widths.append(points - sum(widths))
    offsets = [0, widths[0]]
    chunks = range(len(widths))

    order = ring_order(chips)
    follow = {order[i]: order[(i + 1) % chips] for i in range(chips)}
    ring = [(c * 2 + k, follow[c] * 2 + k) for c in range(chips) for k in range(2)]
    sibling = [(i, i ^ 1) for i in range(band_count)]

    def swap(m):
        return [(i, i ^ (2 * m)) for i in range(band_count)]

    def forward(x):
        return lax.ppermute(x, "band", ring)

    def exchange(x):
        return lax.ppermute(x, "band", sibling)

    own = [
        lax.dynamic_slice_in_dim(conduction, row_index * points + offsets[h], widths[h], 1)
        for h in chunks
    ]
    arrived = [[None] * len(widths) for _ in range(chips)]
    stream = [[None] * len(widths) for _ in range(chips)]
    other = [[None] * len(widths) for _ in range(chips)]
    first = 2 * cond_local
    arrived[1] = [forward(x) for x in own]
    near = nearby(valence_store, QDEV * band_count, own[0])
    nears = [near] + [lax.ppermute(near, "row", [(0, r)]) for r in range(1, row_count)]
    windows, (*arrived[1], stream[0][0], stream[0][1]) = cut(
        valence_store, conduction, nears, chips, arrived[1] + own
    )
    for m in range(1, chips):
        windows[m] = lax.ppermute(windows[m], "band", swap(m))

    def send_on(s, h, carried):
        stream[s][h] = carried
        if s + 1 < chips:
            arrived[s + 1][h] = forward(carried)
        other[s][h] = exchange(carried)

    scale = 4.0 / math.sqrt(cond_local * band_count * NV)
    occupied = occupancy.astype(F32)
    weight = occupied[None, :] / (valence_energy[None, :] - cond_energy[:, None]) * scale
    weight = jnp.pad(weight, ((0, 0), (0, NVPAD - NV)))

    for h in chunks:
        send_on(1, h, arrived[1][h])
    packed, near, stream[0] = pack(owners, windows, first, valence_store.shape[0], stream[0])
    theirs = exchange(packed)
    other[0] = [exchange(x) for x in stream[0]]
    waiting = [(s, h) for s in range(2, chips) for h in chunks]
    s, h = waiting.pop(0)
    (left, values, token), carried = prepare(
        weight, packed, theirs, windows, near, share, first, [arrived[s][h]]
    )
    send_on(s, h, *carried)
    while len(waiting) > 1:
        s, h = waiting.pop(0)
        send_on(s, h, *gate(token, [arrived[s][h]]))

    def part(begin, end, h, acc, out):
        pairs = [(stream[s][h], other[s][h]) for s in range(begin, end)]
        streams = [x for pair in pairs for x in pair]
        return product(begin, end, left, streams, values, acc, offsets[h], out, points)

    early, token = part(0, chips - 2, 1, None, False)
    s, h = waiting.pop(0)
    send_on(s, h, *gate(token, [arrived[s][h]]))
    out, _ = part(0, chips, 0, None, None)
    return part(chips - 2, chips, 1, early, out)[0]


def solution(mesh):
    in_specs = (P("band", "row"), P(), P(), P(), P("band", None), P())
    out_specs = P("band", "row")
    return jax.shard_map(body, mesh=mesh, in_specs=in_specs, out_specs=out_specs, check_vma=False)
```

```python
import math

import jax
import jax.numpy as jnp
from jax import lax
from jax.experimental import pallas as pl
from jax.experimental.pallas import tpu as pltpu
from jax.sharding import PartitionSpec as P

QDEV = 128
VG = 4
NGROUP = 3
SLOTS = 2
NV = 12
NVPAD = 16
KCHIP = 256
LAST = 2
TILE = 512
VMEM_LIMIT = 40 * 2**20
BF16 = jnp.bfloat16
F32 = jnp.float32

HBM = pl.BlockSpec(memory_space=pltpu.HBM)
VMEM = pl.BlockSpec(memory_space=pltpu.VMEM)


def ring_order(chips):
    return [0] + list(range(1, chips, 2)) + list(range(chips - 2, 0, -2))


def previous(chips):
    order = ring_order(chips)
    return [order[order.index(c) - 1] for c in range(chips)]


def lookup(table, index):
    value = jnp.int32(table[0])
    for i in range(1, len(table)):
        value = jnp.where(index == i, jnp.int32(table[i]), value)
    return value


def call(kernel, name, operands, in_specs, out_shape, out_specs, scratch=(), aliases=None, carry=()):
    ins, outs, carried = len(operands), len(out_shape), len(carry)

    def body(*refs):
        rest = refs[ins + carried :]
        kernel(*refs[:ins], *rest[:outs], *rest[outs + carried :])

    aliases = dict(aliases or {})
    for i in range(carried):
        aliases[ins + i] = outs + i
    results = pl.pallas_call(
        body,
        out_shape=list(out_shape) + [jax.ShapeDtypeStruct(x.shape, x.dtype) for x in carry],
        in_specs=list(in_specs) + [VMEM] * carried,
        out_specs=list(out_specs) + [VMEM] * carried,
        scratch_shapes=list(scratch),
        input_output_aliases=aliases,
        compiler_params=pltpu.CompilerParams(vmem_limit_bytes=VMEM_LIMIT),
        name=name,
    )(*operands, *carry)
    return list(results[:outs]), list(results[outs:])


def pinned(x):
    return pltpu.with_memory_space_constraint(x, pltpu.HBM)


def cut(store, conduction, nears, chips, carry):
    slots, points = store.shape
    cond_local = conduction.shape[0]
    first = 2 * cond_local
    blocks = points // QDEV

    def kernel(store_ref, cond_ref, *refs):
        near_refs = refs[: len(nears)]
        refs = refs[len(nears) :]
        outs = refs[:chips]
        rows_ref, sems = refs[chips:]
        chip = lax.axis_index("band") // 2
        copies = [pltpu.make_async_copy(store_ref, rows_ref, sems.at[0])]
        for m in range(chips):
            for k in range(2):
                start = ((chip ^ m) * 2 + k) * QDEV
                copies.append(
                    pltpu.make_async_copy(
                        cond_ref.at[:, pl.ds(pl.multiple_of(start, QDEV), QDEV)],
                        outs[m].at[k * cond_local : (k + 1) * cond_local],
                        sems.at[1 + 2 * m + k],
                    )
                )
        for copy in copies:
            copy.start()
        copies[0].wait()
        for block in range(blocks):
            rows = rows_ref[:, block * QDEV : (block + 1) * QDEV]
            for out_ref in outs:
                out_ref[first + block * slots : first + (block + 1) * slots, :] = rows
        for m in range(chips):
            for k in range(2):
                lanes = pl.ds(pl.multiple_of(((chip ^ m) * 2 + k) * QDEV, QDEV), QDEV)
                rows = near_refs[0][:, lanes].astype(F32)
                for ref in near_refs[1:]:
                    rows = rows + ref[:, lanes].astype(F32)
                start = first + (blocks + k) * slots
                outs[m][start : start + slots, :] = rows.astype(BF16)
        for copy in copies[1:]:
            copy.wait()

    shape = jax.ShapeDtypeStruct((first + (blocks + 2) * slots, QDEV), BF16)
    return call(
        kernel,
        "cut",
        [pinned(store), pinned(conduction)] + nears,
        [HBM] * 2 + [VMEM] * len(nears),
        [shape] * chips,
        [VMEM] * chips,
        [pltpu.VMEM(store.shape, BF16), pltpu.SemaphoreType.DMA((1 + 2 * chips,))],
        carry=carry,
    )


def pack(owners, windows, first, slots, carry):
    chips = len(windows)
    cond_local = first // 2
    blocks = (windows[0].shape[0] - first) // slots - 2
    share = blocks * NV

    def kernel(owners_ref, *refs):
        window_refs = refs[:chips]
        out_ref, near_ref, group_ref, sem = refs[chips:]
        copy = pltpu.make_async_copy(owners_ref, group_ref, sem)
        copy.start()
        band = lax.axis_index("band")
        core = band % 2
        for m in range(chips):
            start = pl.multiple_of((1 - core) * cond_local, 16)
            out_ref[share + m * cond_local : share + (m + 1) * cond_local] = window_refs[m][
                pl.ds(start, cond_local)
            ]
        copy.wait()
        def chosen(start):
            rows = [ref[pl.ds(start, slots), :].astype(F32) for ref in window_refs]
            parts = []
            for group in range(NGROUP):
                at = group % SLOTS * VG
                part = jnp.zeros((VG, QDEV), F32)
                for m in range(chips):
                    source = band ^ (2 * m)
                    part = jnp.where(source == group_ref[group], rows[m][at : at + VG], part)
                parts.append(part)
            return parts

        for block in range(blocks):
            rows = jnp.concatenate(chosen(first + block * slots), axis=0)
            out_ref[block * NV : (block + 1) * NV] = rows.astype(BF16)
        rest = [jnp.zeros((NVPAD - NV, QDEV), F32)]
        near = first + blocks * slots
        mine = jnp.concatenate(chosen(pl.multiple_of(near + core * slots, 8)) + rest, axis=0)
        near_ref[...] = mine.astype(BF16)
        theirs = jnp.concatenate(chosen(pl.multiple_of(near + (1 - core) * slots, 8)) + rest, axis=0)
        out_ref[share + chips * cond_local :] = theirs.astype(BF16)

    (packed, near), carried = call(
        kernel,
        "pack",
        [pinned(owners)] + windows,
        [HBM] + [VMEM] * chips,
        [
            jax.ShapeDtypeStruct((share + chips * cond_local + NVPAD, QDEV), BF16),
            jax.ShapeDtypeStruct((NVPAD, QDEV), BF16),
        ],
        [VMEM] * 2,
        [pltpu.SMEM(owners.shape, jnp.int32), pltpu.SemaphoreType.DMA],
        carry=carry,
    )
    return packed, near, carried


def nearby(store, window, lead):
    def kernel(store_ref, lead_ref, out_ref, sem):
        copy = pltpu.make_async_copy(store_ref.at[:, :window], out_ref, sem)
        copy.start()
        copy.wait()

        @pl.when(lax.axis_index("row") != 0)
        def _():
            out_ref[...] = jnp.zeros_like(out_ref)

    shape = jax.ShapeDtypeStruct((store.shape[0], window), BF16)
    outs, _ = call(
        kernel,
        "nearby",
        [pinned(store), lead],
        [HBM, VMEM],
        [shape],
        [VMEM],
        [pltpu.SemaphoreType.DMA],
    )
    return outs[0]


def gate(token, carry):
    def kernel(token_ref):
        pass

    return call(kernel, "gate", [token], [VMEM], [], [], carry=carry)[1]


def sources(chip, chips):
    before = previous(chips)
    found = [chip]
    for _ in range(chips - 1):
        found.append(lookup(before, found[-1]))
    return found


def prepare(weight, packed, got, windows, near, share, first, carry):
    chips = len(windows)
    cond_local = first // 2
    blocks = share // NV
    depth = chips * first

    def kernel(weight_ref, packed_ref, got_ref, near_ref, *refs):
        window_refs = refs[:chips]
        left_ref, values_ref, token_ref, cols_ref = refs[chips:]
        token_ref[...] = jnp.zeros_like(token_ref)
        band = lax.axis_index("band")
        chip = band // 2
        core = band % 2
        for block in range(blocks):
            rows = slice(block * NV, (block + 1) * NV)
            values = packed_ref[rows].astype(F32) + got_ref[rows].astype(F32)
            values_ref[:NV, block * QDEV : (block + 1) * QDEV] = values
        steps = sources(chip, chips)
        parts = []
        for source in steps:
            for k in (core, 1 - core):
                start = source * first + k * cond_local
                parts.append(weight_ref[pl.ds(pl.multiple_of(start, 8), cond_local), :])
        weights = jnp.concatenate(parts, axis=0).T
        for m in range(chips):
            step = jnp.int32(0)
            for s in range(1, chips):
                step = jnp.where(steps[s] == (chip ^ m), jnp.int32(s), step)
            base = step * first
            mine = core * cond_local
            cols_ref[pl.ds(pl.multiple_of(base, 16), cond_local)] = window_refs[m][
                pl.ds(pl.multiple_of(mine, 16), cond_local)
            ].astype(F32)
            theirs = slice(share + m * cond_local, share + (m + 1) * cond_local)
            cols_ref[pl.ds(pl.multiple_of(base + cond_local, 16), cond_local)] = got_ref[
                theirs
            ].astype(F32)
        near = near_ref[...].astype(F32) + got_ref[share + chips * cond_local :].astype(F32)
        near = near.T
        cond = cols_ref[...].T
        for v in range(NV):
            left = (near[:, v : v + 1] * cond) * weights[v : v + 1, :]
            high = left.astype(BF16)
            low = (left - high.astype(F32)).astype(BF16)
            rows = slice(v * QDEV, (v + 1) * QDEV)
            left_ref[rows, :depth] = high
            left_ref[rows, depth:] = low

    return call(
        kernel,
        "prep",
        [weight, packed, got, near] + windows,
        [VMEM] * (4 + chips),
        [
            jax.ShapeDtypeStruct((NV * QDEV, 2 * depth), BF16),
            jax.ShapeDtypeStruct((NVPAD, blocks * QDEV), F32),
            jax.ShapeDtypeStruct((8, 128), F32),
        ],
        [VMEM] * 3,
        [pltpu.VMEM((depth, QDEV), F32)],
        carry=carry,
    )


def product(begin, end, left, streams, values, acc, offset, out, points):
    count = len(streams)
    cond_local, width = streams[0].shape
    tiles = width // TILE
    half = left.shape[1] // 2
    start = 2 * begin * cond_local // QDEV * QDEV
    stop = -(-2 * end * cond_local // QDEV) * QDEV
    head = 2 * begin * cond_local - start
    tail = stop - 2 * end * cond_local
    final = out is not False

    def kernel(left_ref, values_ref, *refs):
        stream_refs = refs[:count]
        rest = list(refs[count:])
        acc_ref = None if acc is None else rest.pop(0)
        if final and out is not None:
            rest.pop(0)
        out_ref, token_ref = rest[:2]
        token_ref[...] = jnp.zeros_like(token_ref)
        copies = []
        for tile in range(tiles):
            lanes = slice(tile * TILE, (tile + 1) * TILE)
            at = slice(offset + tile * TILE, offset + (tile + 1) * TILE)
            parts = [ref[:, lanes] for ref in stream_refs]
            if head:
                parts = [jnp.zeros((head, TILE), BF16)] + parts
            if tail:
                parts = parts + [jnp.zeros((tail, TILE), BF16)]
            right = jnp.concatenate(parts + parts, axis=0)
            total = None if acc is None else acc_ref[:, lanes]
            for v in range(0, NV, VG):
                rows = slice(v * QDEV, (v + VG) * QDEV)
                lhs = jnp.concatenate(
                    [left_ref[rows, start:stop], left_ref[rows, half + start : half + stop]], axis=1
                )
                m = jnp.dot(lhs, right, preferred_element_type=F32)
                for j in range(VG):
                    term = m[j * QDEV : (j + 1) * QDEV] * values_ref[v + j : v + j + 1, at]
                    total = term if total is None else total + term
            if final:
                stage_ref, sems = rest[2:]
                stage_ref[tile] = total
                copy = pltpu.make_async_copy(stage_ref.at[tile], out_ref.at[:, at], sems.at[tile])
                copy.start()
                copies.append(copy)
            else:
                out_ref[:, lanes] = total
        for copy in copies:
            copy.wait()

    operands = [left, values] + streams
    in_specs = [VMEM] * len(operands)
    aliases = {}
    scratch = []
    if acc is not None:
        operands.append(acc)
        in_specs.append(VMEM)
    if final:
        if out is not None:
            operands.append(out)
            in_specs.append(HBM)
            aliases = {len(operands) - 1: 0}
        scratch = [pltpu.VMEM((tiles, QDEV, TILE), F32), pltpu.SemaphoreType.DMA((tiles,))]
    shape = (QDEV, points if final else width)
    outs, _ = call(
        kernel,
        "product",
        operands,
        in_specs,
        [jax.ShapeDtypeStruct(shape, F32), jax.ShapeDtypeStruct((8, 128), F32)],
        [HBM if final else VMEM, VMEM],
        scratch,
        aliases,
    )
    return outs


def body(valence_store, valence_energy, owners, occupancy, conduction, cond_energy):
    band_count = lax.axis_size("band")
    row_count = lax.axis_size("row")
    row_index = lax.axis_index("row")
    chips = band_count // 2
    points = valence_store.shape[1]
    cond_local = conduction.shape[0]
    share = points // QDEV * NV

    units = points // TILE
    widths = [TILE * (units - units // LAST)]
    widths.append(points - sum(widths))
    offsets = [0, widths[0]]
    chunks = range(len(widths))

    order = ring_order(chips)
    follow = {order[i]: order[(i + 1) % chips] for i in range(chips)}
    ring = [(c * 2 + k, follow[c] * 2 + k) for c in range(chips) for k in range(2)]
    sibling = [(i, i ^ 1) for i in range(band_count)]

    def swap(m):
        return [(i, i ^ (2 * m)) for i in range(band_count)]

    def forward(x):
        return lax.ppermute(x, "band", ring)

    def exchange(x):
        return lax.ppermute(x, "band", sibling)

    own = [
        lax.dynamic_slice_in_dim(conduction, row_index * points + offsets[h], widths[h], 1)
        for h in chunks
    ]
    arrived = [[None] * len(widths) for _ in range(chips)]
    stream = [[None] * len(widths) for _ in range(chips)]
    other = [[None] * len(widths) for _ in range(chips)]
    first = 2 * cond_local
    arrived[1] = [forward(x) for x in own]
    near = nearby(valence_store, QDEV * band_count, own[0])
    nears = [near] + [lax.ppermute(near, "row", [(0, r)]) for r in range(1, row_count)]
    windows, (*arrived[1], stream[0][0], stream[0][1]) = cut(
        valence_store, conduction, nears, chips, arrived[1] + own
    )
    for m in range(1, chips):
        windows[m] = lax.ppermute(windows[m], "band", swap(m))

    def send_on(s, h, carried):
        stream[s][h] = carried
        if s + 1 < chips:
            arrived[s + 1][h] = forward(carried)
        other[s][h] = exchange(carried)

    scale = 4.0 / math.sqrt(cond_local * band_count * NV)
    occupied = occupancy.astype(F32)
    weight = occupied[None, :] / (valence_energy[None, :] - cond_energy[:, None]) * scale
    weight = jnp.pad(weight, ((0, 0), (0, NVPAD - NV)))

    for h in chunks:
        send_on(1, h, arrived[1][h])
    packed, near, stream[0] = pack(owners, windows, first, valence_store.shape[0], stream[0])
    theirs = exchange(packed)
    other[0] = [exchange(x) for x in stream[0]]
    waiting = [(s, h) for s in range(2, chips) for h in chunks]
    s, h = waiting.pop(0)
    (left, values, token), carried = prepare(
        weight, packed, theirs, windows, near, share, first, [arrived[s][h]]
    )
    send_on(s, h, *carried)
    while len(waiting) > 3:
        s, h = waiting.pop(0)
        send_on(s, h, *gate(token, [arrived[s][h]]))

    def part(begin, end, h, acc, out):
        pairs = [(stream[s][h], other[s][h]) for s in range(begin, end)]
        streams = [x for pair in pairs for x in pair]
        return product(begin, end, left, streams, values, acc, offsets[h], out, points)

    first_acc, token = part(0, chips - 2, 0, None, False)
    s, h = waiting.pop(0)
    send_on(s, h, *gate(token, [arrived[s][h]]))
    last_acc, token = part(0, chips - 2, 1, None, False)
    for s, h in waiting:
        send_on(s, h, *gate(token, [arrived[s][h]]))
    out, _ = part(chips - 2, chips, 0, first_acc, None)
    return part(chips - 2, chips, 1, last_acc, out)[0]


def solution(mesh):
    in_specs = (P("band", "row"), P(), P(), P(), P("band", None), P())
    out_specs = P("band", "row")
    return jax.shard_map(body, mesh=mesh, in_specs=in_specs, out_specs=out_specs, check_vma=False)
```

```python
import math

import jax
import jax.numpy as jnp
from jax import lax
from jax.experimental import pallas as pl
from jax.experimental.pallas import tpu as pltpu
from jax.sharding import PartitionSpec as P

QDEV = 128
VG = 4
NGROUP = 3
SLOTS = 2
NV = 12
NVPAD = 16
KCHIP = 256
LAST = (3, 8)
TILE = 512
VMEM_LIMIT = 40 * 2**20
BF16 = jnp.bfloat16
F32 = jnp.float32

HBM = pl.BlockSpec(memory_space=pltpu.HBM)
VMEM = pl.BlockSpec(memory_space=pltpu.VMEM)


def ring_order(chips):
    return [0] + list(range(1, chips, 2)) + list(range(chips - 2, 0, -2))


def previous(chips):
    order = ring_order(chips)
    return [order[order.index(c) - 1] for c in range(chips)]


def lookup(table, index):
    value = jnp.int32(table[0])
    for i in range(1, len(table)):
        value = jnp.where(index == i, jnp.int32(table[i]), value)
    return value


def call(kernel, name, operands, in_specs, out_shape, out_specs, scratch=(), aliases=None, carry=()):
    ins, outs, carried = len(operands), len(out_shape), len(carry)

    def body(*refs):
        rest = refs[ins + carried :]
        kernel(*refs[:ins], *rest[:outs], *rest[outs + carried :])

    aliases = dict(aliases or {})
    for i in range(carried):
        aliases[ins + i] = outs + i
    results = pl.pallas_call(
        body,
        out_shape=list(out_shape) + [jax.ShapeDtypeStruct(x.shape, x.dtype) for x in carry],
        in_specs=list(in_specs) + [VMEM] * carried,
        out_specs=list(out_specs) + [VMEM] * carried,
        scratch_shapes=list(scratch),
        input_output_aliases=aliases,
        compiler_params=pltpu.CompilerParams(vmem_limit_bytes=VMEM_LIMIT),
        name=name,
    )(*operands, *carry)
    return list(results[:outs]), list(results[outs:])


def pinned(x):
    return pltpu.with_memory_space_constraint(x, pltpu.HBM)


def cut(store, conduction, nears, chips, carry):
    slots, points = store.shape
    cond_local = conduction.shape[0]
    first = 2 * cond_local
    blocks = points // QDEV

    def kernel(store_ref, cond_ref, *refs):
        near_refs = refs[: len(nears)]
        refs = refs[len(nears) :]
        outs = refs[:chips]
        rows_ref, sems = refs[chips:]
        chip = lax.axis_index("band") // 2
        copies = [pltpu.make_async_copy(store_ref, rows_ref, sems.at[0])]
        for m in range(chips):
            for k in range(2):
                start = ((chip ^ m) * 2 + k) * QDEV
                copies.append(
                    pltpu.make_async_copy(
                        cond_ref.at[:, pl.ds(pl.multiple_of(start, QDEV), QDEV)],
                        outs[m].at[k * cond_local : (k + 1) * cond_local],
                        sems.at[1 + 2 * m + k],
                    )
                )
        for copy in copies:
            copy.start()
        copies[0].wait()
        for block in range(blocks):
            rows = rows_ref[:, block * QDEV : (block + 1) * QDEV]
            for out_ref in outs:
                out_ref[first + block * slots : first + (block + 1) * slots, :] = rows
        for m in range(chips):
            for k in range(2):
                lanes = pl.ds(pl.multiple_of(((chip ^ m) * 2 + k) * QDEV, QDEV), QDEV)
                rows = near_refs[0][:, lanes].astype(F32)
                for ref in near_refs[1:]:
                    rows = rows + ref[:, lanes].astype(F32)
                start = first + (blocks + k) * slots
                outs[m][start : start + slots, :] = rows.astype(BF16)
        for copy in copies[1:]:
            copy.wait()

    shape = jax.ShapeDtypeStruct((first + (blocks + 2) * slots, QDEV), BF16)
    return call(
        kernel,
        "cut",
        [pinned(store), pinned(conduction)] + nears,
        [HBM] * 2 + [VMEM] * len(nears),
        [shape] * chips,
        [VMEM] * chips,
        [pltpu.VMEM(store.shape, BF16), pltpu.SemaphoreType.DMA((1 + 2 * chips,))],
        carry=carry,
    )


def pack(owners, windows, first, slots, carry):
    chips = len(windows)
    cond_local = first // 2
    blocks = (windows[0].shape[0] - first) // slots - 2
    share = blocks * NV

    def kernel(owners_ref, *refs):
        window_refs = refs[:chips]
        out_ref, near_ref, group_ref, sem = refs[chips:]
        copy = pltpu.make_async_copy(owners_ref, group_ref, sem)
        copy.start()
        band = lax.axis_index("band")
        core = band % 2
        for m in range(chips):
            start = pl.multiple_of((1 - core) * cond_local, 16)
            out_ref[share + m * cond_local : share + (m + 1) * cond_local] = window_refs[m][
                pl.ds(start, cond_local)
            ]
        copy.wait()
        def chosen(start):
            rows = [ref[pl.ds(start, slots), :].astype(F32) for ref in window_refs]
            parts = []
            for group in range(NGROUP):
                at = group % SLOTS * VG
                part = jnp.zeros((VG, QDEV), F32)
                for m in range(chips):
                    source = band ^ (2 * m)
                    part = jnp.where(source == group_ref[group], rows[m][at : at + VG], part)
                parts.append(part)
            return parts

        for block in range(blocks):
            rows = jnp.concatenate(chosen(first + block * slots), axis=0)
            out_ref[block * NV : (block + 1) * NV] = rows.astype(BF16)
        rest = [jnp.zeros((NVPAD - NV, QDEV), F32)]
        near = first + blocks * slots
        mine = jnp.concatenate(chosen(pl.multiple_of(near + core * slots, 8)) + rest, axis=0)
        near_ref[...] = mine.astype(BF16)
        theirs = jnp.concatenate(chosen(pl.multiple_of(near + (1 - core) * slots, 8)) + rest, axis=0)
        out_ref[share + chips * cond_local :] = theirs.astype(BF16)

    (packed, near), carried = call(
        kernel,
        "pack",
        [pinned(owners)] + windows,
        [HBM] + [VMEM] * chips,
        [
            jax.ShapeDtypeStruct((share + chips * cond_local + NVPAD, QDEV), BF16),
            jax.ShapeDtypeStruct((NVPAD, QDEV), BF16),
        ],
        [VMEM] * 2,
        [pltpu.SMEM(owners.shape, jnp.int32), pltpu.SemaphoreType.DMA],
        carry=carry,
    )
    return packed, near, carried


def nearby(store, window, lead):
    def kernel(store_ref, lead_ref, out_ref, sem):
        copy = pltpu.make_async_copy(store_ref.at[:, :window], out_ref, sem)
        copy.start()
        copy.wait()

        @pl.when(lax.axis_index("row") != 0)
        def _():
            out_ref[...] = jnp.zeros_like(out_ref)

    shape = jax.ShapeDtypeStruct((store.shape[0], window), BF16)
    outs, _ = call(
        kernel,
        "nearby",
        [pinned(store), lead],
        [HBM, VMEM],
        [shape],
        [VMEM],
        [pltpu.SemaphoreType.DMA],
    )
    return outs[0]


def gate(token, carry):
    def kernel(token_ref):
        pass

    return call(kernel, "gate", [token], [VMEM], [], [], carry=carry)[1]


def sources(chip, chips):
    before = previous(chips)
    found = [chip]
    for _ in range(chips - 1):
        found.append(lookup(before, found[-1]))
    return found


def prepare(weight, packed, got, windows, near, share, first, carry):
    chips = len(windows)
    cond_local = first // 2
    blocks = share // NV
    depth = chips * first

    def kernel(weight_ref, packed_ref, got_ref, near_ref, *refs):
        window_refs = refs[:chips]
        left_ref, values_ref, token_ref, cols_ref = refs[chips:]
        token_ref[...] = jnp.zeros_like(token_ref)
        band = lax.axis_index("band")
        chip = band // 2
        core = band % 2
        for block in range(blocks):
            rows = slice(block * NV, (block + 1) * NV)
            values = packed_ref[rows].astype(F32) + got_ref[rows].astype(F32)
            values_ref[:NV, block * QDEV : (block + 1) * QDEV] = values
        steps = sources(chip, chips)
        parts = []
        for source in steps:
            for k in (core, 1 - core):
                start = source * first + k * cond_local
                parts.append(weight_ref[pl.ds(pl.multiple_of(start, 8), cond_local), :])
        weights = jnp.concatenate(parts, axis=0).T
        for m in range(chips):
            step = jnp.int32(0)
            for s in range(1, chips):
                step = jnp.where(steps[s] == (chip ^ m), jnp.int32(s), step)
            base = step * first
            mine = core * cond_local
            cols_ref[pl.ds(pl.multiple_of(base, 16), cond_local)] = window_refs[m][
                pl.ds(pl.multiple_of(mine, 16), cond_local)
            ].astype(F32)
            theirs = slice(share + m * cond_local, share + (m + 1) * cond_local)
            cols_ref[pl.ds(pl.multiple_of(base + cond_local, 16), cond_local)] = got_ref[
                theirs
            ].astype(F32)
        near = near_ref[...].astype(F32) + got_ref[share + chips * cond_local :].astype(F32)
        near = near.T
        cond = cols_ref[...].T
        for v in range(NV):
            left = (near[:, v : v + 1] * cond) * weights[v : v + 1, :]
            high = left.astype(BF16)
            low = (left - high.astype(F32)).astype(BF16)
            rows = slice(v * QDEV, (v + 1) * QDEV)
            left_ref[rows, :depth] = high
            left_ref[rows, depth:] = low

    return call(
        kernel,
        "prep",
        [weight, packed, got, near] + windows,
        [VMEM] * (4 + chips),
        [
            jax.ShapeDtypeStruct((NV * QDEV, 2 * depth), BF16),
            jax.ShapeDtypeStruct((NVPAD, blocks * QDEV), F32),
            jax.ShapeDtypeStruct((8, 128), F32),
        ],
        [VMEM] * 3,
        [pltpu.VMEM((depth, QDEV), F32)],
        carry=carry,
    )


def product(begin, end, left, streams, values, acc, offset, out, points):
    count = len(streams)
    cond_local, width = streams[0].shape
    tiles = width // TILE
    half = left.shape[1] // 2
    start = 2 * begin * cond_local // QDEV * QDEV
    stop = -(-2 * end * cond_local // QDEV) * QDEV
    head = 2 * begin * cond_local - start
    tail = stop - 2 * end * cond_local
    final = out is not False

    def kernel(left_ref, values_ref, *refs):
        stream_refs = refs[:count]
        rest = list(refs[count:])
        acc_ref = None if acc is None else rest.pop(0)
        if final and out is not None:
            rest.pop(0)
        out_ref, token_ref = rest[:2]
        token_ref[...] = jnp.zeros_like(token_ref)
        copies = []
        for tile in range(tiles):
            lanes = slice(tile * TILE, (tile + 1) * TILE)
            at = slice(offset + tile * TILE, offset + (tile + 1) * TILE)
            parts = [ref[:, lanes] for ref in stream_refs]
            if head:
                parts = [jnp.zeros((head, TILE), BF16)] + parts
            if tail:
                parts = parts + [jnp.zeros((tail, TILE), BF16)]
            right = jnp.concatenate(parts + parts, axis=0)
            total = None if acc is None else acc_ref[:, lanes]
            for v in range(0, NV, VG):
                rows = slice(v * QDEV, (v + VG) * QDEV)
                lhs = jnp.concatenate(
                    [left_ref[rows, start:stop], left_ref[rows, half + start : half + stop]], axis=1
                )
                m = jnp.dot(lhs, right, preferred_element_type=F32)
                for j in range(VG):
                    term = m[j * QDEV : (j + 1) * QDEV] * values_ref[v + j : v + j + 1, at]
                    total = term if total is None else total + term
            if final:
                stage_ref, sems = rest[2:]
                stage_ref[tile] = total
                copy = pltpu.make_async_copy(stage_ref.at[tile], out_ref.at[:, at], sems.at[tile])
                copy.start()
                copies.append(copy)
            else:
                out_ref[:, lanes] = total
        for copy in copies:
            copy.wait()

    operands = [left, values] + streams
    in_specs = [VMEM] * len(operands)
    aliases = {}
    scratch = []
    if acc is not None:
        operands.append(acc)
        in_specs.append(VMEM)
    if final:
        if out is not None:
            operands.append(out)
            in_specs.append(HBM)
            aliases = {len(operands) - 1: 0}
        scratch = [pltpu.VMEM((tiles, QDEV, TILE), F32), pltpu.SemaphoreType.DMA((tiles,))]
    shape = (QDEV, points if final else width)
    outs, _ = call(
        kernel,
        "product",
        operands,
        in_specs,
        [jax.ShapeDtypeStruct(shape, F32), jax.ShapeDtypeStruct((8, 128), F32)],
        [HBM if final else VMEM, VMEM],
        scratch,
        aliases,
    )
    return outs


def body(valence_store, valence_energy, owners, occupancy, conduction, cond_energy):
    band_count = lax.axis_size("band")
    row_count = lax.axis_size("row")
    row_index = lax.axis_index("row")
    chips = band_count // 2
    points = valence_store.shape[1]
    cond_local = conduction.shape[0]
    share = points // QDEV * NV

    units = points // TILE
    widths = [TILE * (units - units * LAST[0] // LAST[1])]
    widths.append(points - sum(widths))
    offsets = [0, widths[0]]
    chunks = range(len(widths))

    order = ring_order(chips)
    follow = {order[i]: order[(i + 1) % chips] for i in range(chips)}
    ring = [(c * 2 + k, follow[c] * 2 + k) for c in range(chips) for k in range(2)]
    sibling = [(i, i ^ 1) for i in range(band_count)]

    def swap(m):
        return [(i, i ^ (2 * m)) for i in range(band_count)]

    def forward(x):
        return lax.ppermute(x, "band", ring)

    def exchange(x):
        return lax.ppermute(x, "band", sibling)

    own = [
        lax.dynamic_slice_in_dim(conduction, row_index * points + offsets[h], widths[h], 1)
        for h in chunks
    ]
    arrived = [[None] * len(widths) for _ in range(chips)]
    stream = [[None] * len(widths) for _ in range(chips)]
    other = [[None] * len(widths) for _ in range(chips)]
    first = 2 * cond_local
    arrived[1] = [forward(x) for x in own]
    near = nearby(valence_store, QDEV * band_count, own[0])
    nears = [near] + [lax.ppermute(near, "row", [(0, r)]) for r in range(1, row_count)]
    windows, (*arrived[1], stream[0][0], stream[0][1]) = cut(
        valence_store, conduction, nears, chips, arrived[1] + own
    )
    for m in range(1, chips):
        windows[m] = lax.ppermute(windows[m], "band", swap(m))

    def send_on(s, h, carried):
        stream[s][h] = carried
        if s + 1 < chips:
            arrived[s + 1][h] = forward(carried)
        other[s][h] = exchange(carried)

    scale = 4.0 / math.sqrt(cond_local * band_count * NV)
    occupied = occupancy.astype(F32)
    weight = occupied[None, :] / (valence_energy[None, :] - cond_energy[:, None]) * scale
    weight = jnp.pad(weight, ((0, 0), (0, NVPAD - NV)))

    for h in chunks:
        send_on(1, h, arrived[1][h])
    packed, near, stream[0] = pack(owners, windows, first, valence_store.shape[0], stream[0])
    theirs = exchange(packed)
    other[0] = [exchange(x) for x in stream[0]]
    waiting = [(s, h) for s in range(2, chips) for h in chunks]
    s, h = waiting.pop(0)
    (left, values, token), carried = prepare(
        weight, packed, theirs, windows, near, share, first, [arrived[s][h]]
    )
    send_on(s, h, *carried)
    while len(waiting) > 3:
        s, h = waiting.pop(0)
        send_on(s, h, *gate(token, [arrived[s][h]]))

    def part(begin, end, h, acc, out):
        pairs = [(stream[s][h], other[s][h]) for s in range(begin, end)]
        streams = [x for pair in pairs for x in pair]
        return product(begin, end, left, streams, values, acc, offsets[h], out, points)

    first_acc, token = part(0, chips - 2, 0, None, False)
    s, h = waiting.pop(0)
    send_on(s, h, *gate(token, [arrived[s][h]]))
    last_acc, token = part(0, chips - 2, 1, None, False)
    for s, h in waiting:
        send_on(s, h, *gate(token, [arrived[s][h]]))
    out, _ = part(chips - 2, chips, 0, first_acc, None)
    return part(chips - 2, chips, 1, last_acc, out)[0]


def solution(mesh):
    in_specs = (P("band", "row"), P(), P(), P(), P("band", None), P())
    out_specs = P("band", "row")
    return jax.shard_map(body, mesh=mesh, in_specs=in_specs, out_specs=out_specs, check_vma=False)
```
